512 devices in a mesh: ctx: 16 (over y, core), head: 8 (over z), rep: 4 (over x).
Axes of the slice: x: 4, y: 8, z: 8, core: 2. Of those that a mesh axis runs over, the one named last changes fastest.
Arguments:
- q_turn: bfloat16 [1024, 8192], P(('rep', 'ctx', 'head')), parts along dimension 0, may hold values from -18 to 18
- k_turn: bfloat16 [1024, 1024], P(('rep', 'ctx', 'head')), parts along dimension 0, may hold values from -6 to 6
- v_turn: bfloat16 [1024, 1024], P(('rep', 'ctx', 'head')), parts along dimension 0, may hold values from -6 to 6
- cache_k: bfloat16 [2048, 64, 1024], P(('rep', 'ctx'), None, 'head'), parts along dimension 0, may hold values from -6 to 6
- cache_v: bfloat16 [2048, 64, 1024], P(('rep', 'ctx'), None, 'head'), parts along dimension 0, may hold values from -6 to 6
- k_scale: float32 [2048, 8], P(('rep', 'ctx'), 'head'), parts along dimension 0, may hold values from 0.25 to 2
- v_scale: float32 [2048, 8], P(('rep', 'ctx'), 'head'), parts along dimension 0, may hold values from 0.25 to 2
- page_map: int32 [2048], P(('rep', 'ctx')), parts along dimension 0, may hold values from 0 to 511, as said below
Outputs:
- attn_out: bfloat16 [1024, 8192], P(('rep', 'ctx'), 'head'), parts along dimension 0
- cache_k_paired: bfloat16 [131072, 1024], P(('rep', 'ctx'), 'head'), parts along dimension 0
- cache_v_paired: bfloat16 [131072, 1024], P(('rep', 'ctx'), 'head'), parts along dimension 0
The draws below stay inside these ranges and needn't reach their ends.
There are 4 independent parts, one for each index of `rep`. The reference program is written for one: setup_inputs(seed, part) draws one part's arguments, and reference() takes and returns one part's arrays. A program takes and returns all parts, laid end to end along the dimension named above; each array names one. Nothing has to cross between parts.
Inputs may be any that keep to these rules, and one draw needn't show every extreme that they name: A permutation: slot s holds logical page page_map[s]. Cut the 512 logical pages into 32 blocks of 16 consecutive pages; the 32 slots of each index of ctx hold exactly one page of every block.
All inputs are finite; a program needn't handle non-finite values.
Results may differ from the reference program's by a relative error of at most 0.0087.
Values may be sent and summed in bfloat16 or wider, within the bound.
No kernel may reach another device: no remote copies, remote signals or barrier semaphores. Data moves between devices by JAX's collectives and lax.ppermute only.
A program may use at most 64 MiB of HBM per device.

```python
import math
import jax
import jax.numpy as jnp
from jax import lax

HQ = 64
KVH = 8
HD = 128
PAGE = 64
TURN = 256
PG_DEV = 32
PAGES = 512
CACHE = 32768
N_CTX = 16


def turn_arrays(key):
    base = jax.random.fold_in(key, 21)
    key_query, key_keys = jax.random.split(base, 2)
    queries = jax.random.truncated_normal(key_query, -6.0, 6.0, (TURN, HQ * HD), jnp.float32)
    turn_keys = jax.random.truncated_normal(key_keys, -6.0, 6.0, (TURN, KVH * HD), jnp.float32)
    return (queries, turn_keys)


def draw_q_turn(key, part):
    queries, turn_keys = turn_arrays(key)
    return queries.astype(jnp.bfloat16)


def draw_k_turn(key, part):
    queries, turn_keys = turn_arrays(key)
    return turn_keys.astype(jnp.bfloat16)


def one_ranking(block_key):
    return jax.random.permutation(block_key, PG_DEV // 2)


def draw_page_map(key, part):
    per_device = PG_DEV // (2 * N_CTX)
    block_keys = jax.random.split(jax.random.fold_in(key, 11), 2 * N_CTX)
    ranks = jax.vmap(one_ranking)(block_keys)
    holder = (ranks // per_device).reshape(PAGES).astype(jnp.int32)
    breaker = jax.random.permutation(jax.random.fold_in(key, 12), PAGES).astype(jnp.int32)
    return jnp.argsort(holder * PAGES + breaker).astype(jnp.int32)


def levels(own_key, shape, shards, smallest, top_value):
    def one(position, shards_of):
        heights = jax.random.uniform(jax.random.fold_in(jax.random.fold_in(own_key, 6), position), (shards_of,), jnp.float32, smallest / len(shards), top_value / len(shards))
        return jnp.repeat(jnp.exp(heights), shape[position] // shards_of).reshape((-1,) + (1,) * (len(shape) - position - 1))

    loudness = one(*shards[0])
    for cut in shards[1:]:
        loudness = loudness * one(*cut)
    return loudness


def normal_values(key, shape, scale, bound, cuts=(), kind=jnp.bfloat16):
    result = scale * jax.random.normal(key, shape, jnp.float32)
    if cuts:
        result = result * levels(key, shape, cuts, -0.22, 0.18)
    return jnp.clip(result, -bound, bound).astype(kind)


def setup_inputs(seed: int = 0, part: int = 0) -> dict:
    keys = jax.random.split(jax.random.key(seed), 9)
    part_splits = jax.random.split(jax.random.fold_in(keys[8], part), 9)
    return {
        "q_turn": draw_q_turn(jax.random.fold_in(jax.random.fold_in(keys[8], part), 71), part),
        "k_turn": draw_k_turn(jax.random.fold_in(jax.random.fold_in(keys[8], part), 71), part),
        "v_turn": normal_values(part_splits[2], (TURN, KVH * HD), 1.0, 6.0, ((0, 128),)),
        "cache_k": normal_values(part_splits[3], (PAGES, PAGE, KVH * HD), 1.0, 6.0, ((0, 16), (2, 8))),
        "cache_v": normal_values(part_splits[4], (PAGES, PAGE, KVH * HD), 1.0, 6.0, ((0, 16), (2, 8))),
        "k_scale": jnp.clip(jnp.exp(math.log(2.0) - 2.0794415 * jax.random.uniform(part_splits[5], (PAGES, KVH), jnp.float32) ** levels(part_splits[5], (PAGES, KVH), ((0, 16), (1, 8)), -0.2, 0.2)), 0.25, 2.0),
        "v_scale": jnp.clip(jnp.exp(math.log(2.0) - 2.0794415 * jax.random.uniform(part_splits[6], (PAGES, KVH), jnp.float32) ** levels(part_splits[6], (PAGES, KVH), ((0, 16), (1, 8)), -0.2, 0.2)), 0.25, 2.0),
        "page_map": draw_page_map(jax.random.fold_in(jax.random.fold_in(keys[8], part), 71), part),
    }


def scale_pages(codes, scales):
    full = codes.astype(jnp.float32).reshape(PAGES, PAGE, KVH, HD) * scales[:, None, :, None]
    return full.reshape(PAGES, PAGE, KVH * HD).astype(jnp.bfloat16)

def reference(q_turn, k_turn, v_turn, cache_k, cache_v, k_scale, v_scale, page_map):
    inverse = jnp.argsort(page_map)
    logical_k = scale_pages(cache_k, k_scale)[inverse].reshape(CACHE, KVH * HD)
    logical_v = scale_pages(cache_v, v_scale)[inverse].reshape(CACHE, KVH * HD)
    blocks = 2 * N_CTX
    block_rows = CACHE // blocks
    lower = jnp.arange(N_CTX)
    order = jnp.stack([lower, blocks - 1 - lower], axis=1).reshape(blocks)
    paired_k = logical_k.reshape(blocks, block_rows, KVH * HD)[order].reshape(CACHE, KVH * HD)
    paired_v = logical_v.reshape(blocks, block_rows, KVH * HD)[order].reshape(CACHE, KVH * HD)
    per_group = HQ // KVH
    factor = 1.0 / math.sqrt(HD)
    by_head = q_turn.reshape(TURN, HQ, HD).transpose(1, 0, 2)
    cache_kh = logical_k.reshape(CACHE, KVH, HD)
    cache_vh = logical_v.reshape(CACHE, KVH, HD)
    turn_kh = k_turn.reshape(TURN, KVH, HD)
    turn_vh = v_turn.reshape(TURN, KVH, HD)
    visible = jnp.arange(TURN)[None, :] <= jnp.arange(TURN)[:, None]
    dims = (((1,), (1,)), ((), ()))

    def one_head(pair):
        query, index = pair
        kv_index = index // per_group
        ck = lax.dynamic_index_in_dim(cache_kh, kv_index, 1, keepdims=False)
        cv = lax.dynamic_index_in_dim(cache_vh, kv_index, 1, keepdims=False)
        tk = lax.dynamic_index_in_dim(turn_kh, kv_index, 1, keepdims=False)
        tv = lax.dynamic_index_in_dim(turn_vh, kv_index, 1, keepdims=False)
        cached = lax.dot_general(query, ck, dims, preferred_element_type=jnp.float32) * factor
        recent = lax.dot_general(query, tk, dims, preferred_element_type=jnp.float32) * factor
        recent = jnp.where(visible, recent, -jnp.inf)
        peak = jnp.maximum(lax.optimization_barrier(jnp.max(cached, axis=1)), lax.optimization_barrier(jnp.max(recent, axis=1)))
        cached_e = jnp.exp(cached - peak[:, None])
        recent_e = jnp.exp(recent - peak[:, None])
        total = lax.optimization_barrier(jnp.sum(cached_e, axis=1)) + lax.optimization_barrier(jnp.sum(recent_e, axis=1))
        mixed = jnp.dot(cached_e.astype(jnp.bfloat16), cv, preferred_element_type=jnp.float32)
        mixed = mixed + jnp.dot(recent_e.astype(jnp.bfloat16), tv, preferred_element_type=jnp.float32)
        return mixed / total[:, None]
    heads_out = lax.map(one_head, (by_head, jnp.arange(HQ, dtype=jnp.int32)))
    attn_out = heads_out.transpose(1, 0, 2).reshape(TURN, HQ * HD).astype(jnp.bfloat16)
    return (attn_out, paired_k, paired_v)
```

```python
import math

import jax
import jax.numpy as jnp
from jax import lax
from jax.experimental import pallas as pl
from jax.experimental.pallas import tpu as pltpu
from jax.sharding import PartitionSpec as P


INFO_ROWS = 8
BF16 = jnp.bfloat16
F32 = jnp.float32


def prepare_kernel(map_ref, k_scale_ref, v_scale_ref, k_ref, v_ref, send_ref, *, half, peers):
    slots, page_rows, width = k_ref.shape
    body_rows = 4 * page_rows
    row = lax.broadcasted_iota(jnp.int32, (INFO_ROWS, width), 0)

    def one_slot(slot, carry):
        page = map_ref[slot]
        block = page // half
        place = page - block * half
        upper = block >= peers
        owner = jnp.where(upper, 2 * peers - 1 - block, block)
        side = jnp.where(upper, 1, 0)
        at_k = pl.multiple_of(side * page_rows, page_rows)
        at_v = pl.multiple_of((2 + side) * page_rows, page_rows)
        send_ref[owner, pl.ds(at_k, page_rows), :] = (
            k_ref[slot].astype(F32) * k_scale_ref[slot]
        ).astype(BF16)
        send_ref[owner, pl.ds(at_v, page_rows), :] = (
            v_ref[slot].astype(F32) * v_scale_ref[slot]
        ).astype(BF16)
        info = send_ref[owner, body_rows : body_rows + INFO_ROWS, :].astype(F32)
        info = jnp.where(row == side, place.astype(F32), info)
        send_ref[owner, body_rows : body_rows + INFO_ROWS, :] = info.astype(BF16)
        return carry

    send_ref[:, body_rows:, :] = jnp.zeros((peers, INFO_ROWS, width), BF16)
    lax.fori_loop(0, slots, one_slot, 0)


def place_kernel(info_ref, recv_ref, k_ref, v_ref, *, half, page_rows):
    peers = recv_ref.shape[0]

    def one_peer(peer, carry):
        for side in range(2):
            at = info_ref[2 * peer + side] * page_rows + side * half * page_rows
            at = pl.multiple_of(at, page_rows)
            k_ref[pl.ds(at, page_rows), :] = recv_ref[peer, pl.ds(side * page_rows, page_rows), :]
            v_ref[pl.ds(at, page_rows), :] = recv_ref[
                peer, pl.ds((2 + side) * page_rows, page_rows), :
            ]
        return carry

    lax.fori_loop(0, peers, one_peer, 0)


def attend_kernel(
    start_ref, q_ref, kv_ref, tk_ref, tv_ref, msg_ref, s_even, s_odd, stat_ref, *, factor, keys_at_once
):
    peers, _, dim = kv_ref.shape
    length, width = q_ref.shape
    heads = width // dim
    own = tk_ref.shape[0]
    kv_rows = (kv_ref.shape[1] - INFO_ROWS) // 2
    per_chunk = keys_at_once // kv_rows
    chunks = peers // per_chunk
    log_factor = factor * math.log2(math.e)
    contract = (((1,), (1,)), ((), ()))
    lane = lax.broadcasted_iota(jnp.int32, (length, dim), 1)
    token = lax.broadcasted_iota(jnp.int32, (length, own), 0)
    turn_key = start_ref[0] + lax.broadcasted_iota(jnp.int32, (length, own), 1)
    visible = turn_key <= token

    def scores(head, s_ref):
        query = q_ref[:, head * dim : (head + 1) * dim]
        peak = None
        for c in range(chunks):
            keys = kv_ref[c * per_chunk : (c + 1) * per_chunk, 0:kv_rows, :].reshape(keys_at_once, dim)
            s = lax.dot_general(query, keys, contract, preferred_element_type=F32)
            s_ref[:, c * keys_at_once : (c + 1) * keys_at_once] = s
            for i in range(keys_at_once // dim):
                part = s[:, i * dim : (i + 1) * dim]
                peak = part if peak is None else jnp.maximum(peak, part)
        recent = lax.dot_general(query, tk_ref[...], contract, preferred_element_type=F32)
        recent = jnp.where(visible, recent, -jnp.inf)
        top = jnp.maximum(
            jnp.max(peak, axis=1, keepdims=True), jnp.max(recent, axis=1, keepdims=True)
        )
        shift = (top * log_factor).astype(BF16).astype(F32)
        return recent, shift

    def weights(head, s_ref, recent, shift):
        e = jnp.exp2(recent * log_factor - shift)
        total = jnp.sum(e, axis=1, keepdims=True)
        mixed = jnp.dot(e.astype(BF16), tv_ref[...], preferred_element_type=F32)
        spread = jnp.broadcast_to(shift, (length, dim))
        sums = None
        for c in range(chunks):
            values = kv_ref[c * per_chunk : (c + 1) * per_chunk, kv_rows : 2 * kv_rows, :].reshape(
                keys_at_once, dim
            )
            parts = []
            for i in range(keys_at_once // dim):
                at = c * keys_at_once + i * dim
                part = jnp.exp2(s_ref[:, at : at + dim] * log_factor - spread)
                sums = part if sums is None else sums + part
                parts.append(part.astype(BF16))
            mixed = mixed + jnp.dot(
                jnp.concatenate(parts, axis=1), values, preferred_element_type=F32
            )
        total = total + jnp.sum(sums, axis=1, keepdims=True)
        high = total.astype(BF16).astype(F32)
        stat = stat_ref[...]
        stat = jnp.where(lane == head, shift, stat)
        stat = jnp.where(lane == heads + head, high, stat)
        stat = jnp.where(lane == 2 * heads + head, total - high, stat)
        stat_ref[...] = stat
        msg_ref[:, head * own : (head + 1) * own, :] = mixed.astype(BF16).reshape(
            peers, own, dim
        )

    stat_ref[...] = jnp.zeros((length, dim), F32)
    held = scores(0, s_even)
    for head in range(heads):
        now, later = (s_even, s_odd) if head % 2 == 0 else (s_odd, s_even)
        coming = scores(head + 1, later) if head + 1 < heads else None
        weights(head, now, *held)
        held = coming
    msg_ref[:, heads * own :, :] = stat_ref[...].astype(BF16).reshape(peers, own, dim)


def combine_kernel(msg_ref, out_ref, *, heads):
    peers, _, dim = msg_ref.shape
    own = out_ref.shape[0]
    stats = [msg_ref[p, heads * own : (heads + 1) * own, :].astype(F32) for p in range(peers)]
    top = stats[0]
    for p in range(1, peers):
        top = jnp.maximum(top, stats[p])
    lane = lax.broadcasted_iota(jnp.int32, (own, dim), 1)
    keep = lane < heads
    factors, total = [], jnp.zeros((own, dim), F32)
    for p in range(peers):
        w = jnp.exp2(jnp.where(keep, stats[p] - top, 0.0))
        sums = pltpu.roll(stats[p], dim - heads, 1) + pltpu.roll(stats[p], dim - 2 * heads, 1)
        total = total + w * sums
        factors.append(w)
    total = jnp.where(keep, total, 1.0)
    factors = [w / total for w in factors]
    for h in range(heads):
        acc = None
        for p in range(peers):
            part = msg_ref[p, h * own : (h + 1) * own, :].astype(F32) * factors[p][:, h : h + 1]
            acc = part if acc is None else acc + part
        out_ref[:, h * dim : (h + 1) * dim] = acc.astype(BF16)


def whole(memory_space=pltpu.VMEM):
    return pl.BlockSpec(memory_space=memory_space)


def step(q_turn, k_turn, v_turn, cache_k, cache_v, k_scale, v_scale, page_map):
    peers = lax.axis_size("ctx")
    groups = lax.axis_size("head")
    position = lax.axis_index("ctx")
    slots, page_rows, dim = cache_k.shape
    half = slots // 2
    tokens = q_turn.shape[0]
    width = q_turn.shape[1] // groups
    heads = width // dim
    smem = whole(pltpu.SMEM)
    vmem = whole()

    turn = jnp.concatenate(
        [a.reshape(tokens, groups, -1) for a in (q_turn, k_turn, v_turn)], axis=2
    )
    turn = lax.all_to_all(turn, "head", split_axis=1, concat_axis=0, tiled=True)
    own = tokens * groups
    turn = turn.reshape(own, width + 2 * dim)
    q_mine = turn[:, :width]
    k_mine = turn[:, width : width + dim]
    v_mine = turn[:, width + dim :]

    queries = lax.all_gather(q_mine, "ctx", axis=0, tiled=True)
    length = queries.shape[0]

    send = pl.pallas_call(
        lambda *refs: prepare_kernel(*refs, half=half, peers=peers),
        out_shape=jax.ShapeDtypeStruct((peers, 4 * page_rows + INFO_ROWS, dim), BF16),
        in_specs=[smem, smem, smem, vmem, vmem],
        out_specs=vmem,
        name="prepare",
    )(page_map, k_scale.reshape(slots), v_scale.reshape(slots), cache_k, cache_v)
    queries, outgoing = lax.optimization_barrier((queries, send))
    recv = lax.all_to_all(outgoing, "ctx", split_axis=0, concat_axis=0, tiled=True)

    keys_at_once = 512
    attend = pl.pallas_call(
        lambda *refs: attend_kernel(*refs, factor=1.0 / math.sqrt(dim), keys_at_once=keys_at_once),
        out_shape=jax.ShapeDtypeStruct((peers, (heads + 1) * own, dim), BF16),
        in_specs=[smem, vmem, vmem, vmem, vmem],
        out_specs=vmem,
        scratch_shapes=[
            pltpu.VMEM((length, slots * page_rows), F32),
            pltpu.VMEM((length, slots * page_rows), F32),
            pltpu.VMEM((length, dim), F32),
        ],
        name="attend",
    )
    start = (position * own).reshape(1).astype(jnp.int32)
    msg = attend(start, queries, send, k_mine, v_mine)
    msg, recv = lax.optimization_barrier((msg, recv))
    parts = lax.all_to_all(msg, "ctx", split_axis=0, concat_axis=0, tiled=True)

    info = recv[:, 4 * page_rows : 4 * page_rows + 2, 0].astype(jnp.int32).reshape(2 * peers)
    paired = jax.ShapeDtypeStruct((slots * page_rows, dim), BF16)
    paired_k, paired_v = pl.pallas_call(
        lambda *refs: place_kernel(*refs, half=half, page_rows=page_rows),
        out_shape=(paired, paired),
        in_specs=[smem, vmem],
        out_specs=(vmem, vmem),
        name="place",
    )(info, recv)
    attn_out = pl.pallas_call(
        lambda *refs: combine_kernel(*refs, heads=heads),
        out_shape=jax.ShapeDtypeStruct((own, width), BF16),
        in_specs=[vmem],
        out_specs=vmem,
        name="combine",
    )(parts)
    return (attn_out, paired_k, paired_v)


def solution(mesh):
    return jax.shard_map(
        step,
        mesh=mesh,
        in_specs=(
            P(("rep", "ctx", "head"), None),
            P(("rep", "ctx", "head"), None),
            P(("rep", "ctx", "head"), None),
            P(("rep", "ctx"), None, "head"),
            P(("rep", "ctx"), None, "head"),
            P(("rep", "ctx"), "head"),
            P(("rep", "ctx"), "head"),
            P(("rep", "ctx")),
        ),
        out_specs=(P(("rep", "ctx"), "head"), P(("rep", "ctx"), "head"), P(("rep", "ctx"), "head")),
        check_vma=False,
    )
```

```python
import math

import jax
import jax.numpy as jnp
from jax import lax
from jax.experimental import pallas as pl
from jax.experimental.pallas import tpu as pltpu
from jax.sharding import PartitionSpec as P


INFO_ROWS = 16
CORES = 2
BF16 = jnp.bfloat16
F32 = jnp.float32


def pack_kernel(q_ref, k_ref, v_ref, out_ref, *, groups):
    dim = k_ref.shape[1] // groups
    share = q_ref.shape[1] // (groups * CORES)
    for group in range(groups):
        keys = k_ref[:, group * dim : (group + 1) * dim]
        values = v_ref[:, group * dim : (group + 1) * dim]
        for core in range(CORES):
            at = (group * CORES + core) * share
            query = q_ref[:, at : at + share]
            for to in range(core * groups + group, out_ref.shape[0], CORES * groups):
                out_ref[to, :, :share] = query
                out_ref[to, :, share : share + dim] = keys
                out_ref[to, :, share + dim :] = values


def prepare_kernel(map_ref, k_scale_ref, v_scale_ref, k_ref, v_ref, send_ref, *, half, peers):
    slots, page_rows, width = k_ref.shape
    body_rows = 4 * page_rows
    row = lax.broadcasted_iota(jnp.int32, (INFO_ROWS, width), 0)

    def one_slot(slot, carry):
        page = map_ref[slot]
        block = page // half
        place = page - block * half
        upper = block >= peers
        owner = jnp.where(upper, 2 * peers - 1 - block, block)
        side = jnp.where(upper, 1, 0)
        at_k = pl.multiple_of(side * page_rows, page_rows)
        at_v = pl.multiple_of((2 + side) * page_rows, page_rows)
        send_ref[owner, pl.ds(at_k, page_rows), :] = (
            k_ref[slot].astype(F32) * k_scale_ref[slot]
        ).astype(BF16)
        send_ref[owner, pl.ds(at_v, page_rows), :] = (
            v_ref[slot].astype(F32) * v_scale_ref[slot]
        ).astype(BF16)
        info = send_ref[owner, body_rows : body_rows + INFO_ROWS, :].astype(F32)
        info = jnp.where(row == side, place.astype(F32), info)
        send_ref[owner, body_rows : body_rows + INFO_ROWS, :] = info.astype(BF16)
        return carry

    send_ref[:, body_rows:, :] = jnp.zeros((peers, INFO_ROWS, width), BF16)
    lax.fori_loop(0, slots, one_slot, 0)


def place_kernel(info_ref, recv_ref, k_ref, v_ref, *, half, page_rows):
    peers = recv_ref.shape[0]

    def one_peer(peer, carry):
        for side in range(2):
            at = info_ref[2 * peer + side] * page_rows + side * half * page_rows
            at = pl.multiple_of(at, page_rows)
            k_ref[pl.ds(at, page_rows), :] = recv_ref[peer, pl.ds(side * page_rows, page_rows), :]
            v_ref[pl.ds(at, page_rows), :] = recv_ref[
                peer, pl.ds((2 + side) * page_rows, page_rows), :
            ]
        return carry

    lax.fori_loop(0, peers, one_peer, 0)


def attend_kernel(
    start_ref, turn_ref, kv_ref, other_ref, msg_ref, s_even, s_odd, stat_ref, *, factor, keys_at_once
):
    peers, _, dim = kv_ref.shape
    length, width = turn_ref.shape
    heads = width // dim - 2
    own = length // peers
    recent_keys = CORES * own
    kv_rows = (kv_ref.shape[1] - INFO_ROWS) // 2
    per_chunk = keys_at_once // kv_rows
    places = [(ref, c) for ref in (kv_ref, other_ref) for c in range(peers // per_chunk)]
    log_factor = factor * math.log2(math.e)
    contract = (((1,), (1,)), ((), ()))
    start = pl.multiple_of(start_ref[0], recent_keys)
    turn_k = turn_ref[pl.ds(start, recent_keys), heads * dim : (heads + 1) * dim]
    turn_v = turn_ref[pl.ds(start, recent_keys), (heads + 1) * dim : (heads + 2) * dim]
    lane = lax.broadcasted_iota(jnp.int32, (length, dim), 1)
    token = lax.broadcasted_iota(jnp.int32, (length, recent_keys), 0)
    turn_key = start + lax.broadcasted_iota(jnp.int32, (length, recent_keys), 1)
    visible = turn_key <= token

    def chunk(place, first_row):
        ref, c = place
        rows = ref[c * per_chunk : (c + 1) * per_chunk, first_row : first_row + kv_rows, :]
        return rows.reshape(keys_at_once, dim)

    def scores(head, s_ref):
        query = turn_ref[:, head * dim : (head + 1) * dim]
        peak = None
        for n, place in enumerate(places):
            s = lax.dot_general(query, chunk(place, 0), contract, preferred_element_type=F32)
            s_ref[:, n * keys_at_once : (n + 1) * keys_at_once] = s
            for i in range(keys_at_once // dim):
                part = s[:, i * dim : (i + 1) * dim]
                peak = part if peak is None else jnp.maximum(peak, part)
        recent = lax.dot_general(query, turn_k, contract, preferred_element_type=F32)
        recent = jnp.where(visible, recent, -jnp.inf)
        top = jnp.maximum(
            jnp.max(peak, axis=1, keepdims=True), jnp.max(recent, axis=1, keepdims=True)
        )
        shift = (top * log_factor).astype(BF16).astype(F32)
        return recent, shift

    def weights(head, s_ref, recent, shift):
        e = jnp.exp2(recent * log_factor - shift)
        total = jnp.sum(e, axis=1, keepdims=True)
        mixed = jnp.dot(e.astype(BF16), turn_v, preferred_element_type=F32)
        spread = jnp.broadcast_to(shift, (length, dim))
        sums = None
        for n, place in enumerate(places):
            parts = []
            for i in range(keys_at_once // dim):
                at = n * keys_at_once + i * dim
                part = jnp.exp2(s_ref[:, at : at + dim] * log_factor - spread)
                sums = part if sums is None else sums + part
                parts.append(part.astype(BF16))
            mixed = mixed + jnp.dot(
                jnp.concatenate(parts, axis=1), chunk(place, kv_rows), preferred_element_type=F32
            )
        total = total + jnp.sum(sums, axis=1, keepdims=True)
        high = total.astype(BF16).astype(F32)
        stat = stat_ref[...]
        stat = jnp.where(lane == head, shift, stat)
        stat = jnp.where(lane == heads + head, high, stat)
        stat = jnp.where(lane == 2 * heads + head, total - high, stat)
        stat_ref[...] = stat
        msg_ref[:, head * own : (head + 1) * own, :] = mixed.astype(BF16).reshape(
            peers, own, dim
        )

    stat_ref[...] = jnp.zeros((length, dim), F32)
    held = scores(0, s_even)
    for head in range(heads):
        now, later = (s_even, s_odd) if head % 2 == 0 else (s_odd, s_even)
        coming = scores(head + 1, later) if head + 1 < heads else None
        weights(head, now, *held)
        held = coming
    msg_ref[:, heads * own :, :] = stat_ref[...].astype(BF16).reshape(peers, own, dim)


def combine_kernel(msg_ref, out_ref):
    peers, rows, dim = msg_ref.shape
    own = out_ref.shape[0]
    heads = rows // own - 1
    keep = lax.broadcasted_iota(jnp.int32, (own, dim), 1) < heads
    for share in range(CORES):
        senders = range(share, peers, CORES)
        stats = [msg_ref[p, heads * own :, :].astype(F32) for p in senders]
        top = stats[0]
        for stat in stats[1:]:
            top = jnp.maximum(top, stat)
        factors, total = [], jnp.zeros((own, dim), F32)
        for stat in stats:
            w = jnp.exp2(jnp.where(keep, stat - top, 0.0))
            sums = pltpu.roll(stat, dim - heads, 1) + pltpu.roll(stat, dim - 2 * heads, 1)
            total = total + w * sums
            factors.append(w)
        total = jnp.where(keep, total, 1.0)
        factors = [w / total for w in factors]
        for h in range(heads):
            acc = None
            for p, w in zip(senders, factors):
                part = msg_ref[p, h * own : (h + 1) * own, :].astype(F32) * w[:, h : h + 1]
                acc = part if acc is None else acc + part
            at = (share * heads + h) * dim
            out_ref[:, at : at + dim] = acc.astype(BF16)


def whole(memory_space=pltpu.VMEM):
    return pl.BlockSpec(memory_space=memory_space)


def step(q_turn, k_turn, v_turn, cache_k, cache_v, k_scale, v_scale, page_map):
    peers = lax.axis_size("ctx")
    groups = lax.axis_size("head")
    position = lax.axis_index("ctx")
    slots, page_rows, dim = cache_k.shape
    half = slots // 2
    tokens = q_turn.shape[0]
    own = tokens * groups
    length = own * peers
    width = q_turn.shape[1] // groups
    share = width // CORES
    heads = share // dim
    smem = whole(pltpu.SMEM)
    vmem = whole()

    turn = pl.pallas_call(
        lambda *refs: pack_kernel(*refs, groups=groups),
        out_shape=jax.ShapeDtypeStruct((peers * groups, tokens, share + 2 * dim), BF16),
        in_specs=[vmem, vmem, vmem],
        out_specs=vmem,
        name="pack",
    )(q_turn, k_turn, v_turn)
    turn = lax.all_to_all(turn, ("ctx", "head"), split_axis=0, concat_axis=0, tiled=True)

    prepare = pl.pallas_call(
        lambda *refs: prepare_kernel(*refs, half=half, peers=peers),
        out_shape=jax.ShapeDtypeStruct((peers, 4 * page_rows + INFO_ROWS, dim), BF16),
        in_specs=[smem, smem, smem, vmem, vmem],
        out_specs=vmem,
        name="prepare",
    )
    send = prepare(page_map, k_scale.reshape(slots), v_scale.reshape(slots), cache_k, cache_v)
    other = lax.ppermute(send, "ctx", [(i, i ^ 1) for i in range(peers)])
    turn, other, outgoing = lax.optimization_barrier((turn, other, send))
    turn = turn.reshape(length, share + 2 * dim)
    recv = lax.all_to_all(outgoing, "ctx", split_axis=0, concat_axis=0, tiled=True)

    attend = pl.pallas_call(
        lambda *refs: attend_kernel(*refs, factor=1.0 / math.sqrt(dim), keys_at_once=512),
        out_shape=jax.ShapeDtypeStruct((peers, (heads + 1) * own, dim), BF16),
        in_specs=[smem, vmem, vmem, vmem],
        out_specs=vmem,
        scratch_shapes=[
            pltpu.VMEM((length, CORES * slots * page_rows), F32),
            pltpu.VMEM((length, CORES * slots * page_rows), F32),
            pltpu.VMEM((length, dim), F32),
        ],
        name="attend",
    )
    start = (position // CORES * (CORES * own)).reshape(1).astype(jnp.int32)
    msg = attend(start, turn, send, other)
    msg, recv = lax.optimization_barrier((msg, recv))
    parts = lax.all_to_all(msg, "ctx", split_axis=0, concat_axis=0, tiled=True)

    info = recv[:, 4 * page_rows : 4 * page_rows + 2, 0].astype(jnp.int32).reshape(2 * peers)
    paired = jax.ShapeDtypeStruct((slots * page_rows, dim), BF16)
    paired_k, paired_v = pl.pallas_call(
        lambda *refs: place_kernel(*refs, half=half, page_rows=page_rows),
        out_shape=(paired, paired),
        in_specs=[smem, vmem],
        out_specs=(vmem, vmem),
        name="place",
    )(info, recv)
    attn_out = pl.pallas_call(
        combine_kernel,
        out_shape=jax.ShapeDtypeStruct((own, width), BF16),
        in_specs=[vmem],
        out_specs=vmem,
        name="combine",
    )(parts)
    return (attn_out, paired_k, paired_v)


def solution(mesh):
    return jax.shard_map(
        step,
        mesh=mesh,
        in_specs=(
            P(("rep", "ctx", "head"), None),
            P(("rep", "ctx", "head"), None),
            P(("rep", "ctx", "head"), None),
            P(("rep", "ctx"), None, "head"),
            P(("rep", "ctx"), None, "head"),
            P(("rep", "ctx"), "head"),
            P(("rep", "ctx"), "head"),
            P(("rep", "ctx")),
        ),
        out_specs=(P(("rep", "ctx"), "head"), P(("rep", "ctx"), "head"), P(("rep", "ctx"), "head")),
        check_vma=False,
    )
```

```python
import math

import jax
import jax.numpy as jnp
from jax import lax
from jax.experimental import pallas as pl
from jax.experimental.pallas import tpu as pltpu
from jax.sharding import Mesh, PartitionSpec as P


INFO_ROWS = 16
CORES = 2
BF16 = jnp.bfloat16
F32 = jnp.float32
SMALL = pltpu.CompilerParams(vmem_limit_bytes=16 << 20)


def pack_kernel(q_ref, k_ref, v_ref, out_ref, *, groups):
    dim = k_ref.shape[1] // groups
    width = q_ref.shape[1] // groups
    part = width // CORES**2
    for core in range(CORES):
        for group in range(groups):
            to = core * groups + group
            for half in range(CORES):
                at = group * width + (half * CORES + core) * part
                out_ref[to, :, half * part : (half + 1) * part] = q_ref[:, at : at + part]
            at = CORES * part
            out_ref[to, :, at : at + dim] = k_ref[:, group * dim : (group + 1) * dim]
            out_ref[to, :, at + dim :] = v_ref[:, group * dim : (group + 1) * dim]


def fill_kernel(turn_ref, kv_ref, out_ref):
    peers, kv_rows, dim = kv_ref.shape
    tokens = turn_ref.shape[0]
    parts = (out_ref.shape[1] - kv_rows) // tokens
    out_ref[:, :kv_rows, :] = kv_ref[...]
    for core in range(CORES):
        for part in range(parts):
            at = (core * parts + part) * dim
            rows = turn_ref[:, at : at + dim]
            first = kv_rows + part * tokens
            for peer in range(core, peers, CORES):
                out_ref[peer, first : first + tokens, :] = rows


def prepare_kernel(map_ref, k_scale_ref, v_scale_ref, k_ref, v_ref, send_ref, *, half, peers):
    slots, page_rows, width = k_ref.shape
    body_rows = 4 * page_rows
    row = lax.broadcasted_iota(jnp.int32, (INFO_ROWS, width), 0)

    def one_slot(slot, carry):
        page = map_ref[slot]
        block = page // half
        place = page - block * half
        upper = block >= peers
        owner = jnp.where(upper, 2 * peers - 1 - block, block)
        side = jnp.where(upper, 1, 0)
        at_k = pl.multiple_of(side * page_rows, page_rows)
        at_v = pl.multiple_of((2 + side) * page_rows, page_rows)
        send_ref[owner, pl.ds(at_k, page_rows), :] = (
            k_ref[slot].astype(F32) * k_scale_ref[slot]
        ).astype(BF16)
        send_ref[owner, pl.ds(at_v, page_rows), :] = (
            v_ref[slot].astype(F32) * v_scale_ref[slot]
        ).astype(BF16)
        info = send_ref[owner, body_rows : body_rows + INFO_ROWS, :].astype(F32)
        info = jnp.where(row == side, place.astype(F32), info)
        send_ref[owner, body_rows : body_rows + INFO_ROWS, :] = info.astype(BF16)
        return carry

    send_ref[:, body_rows:, :] = jnp.zeros((peers, INFO_ROWS, width), BF16)
    lax.fori_loop(0, slots, one_slot, 0)


def place_kernel(info_ref, recv_ref, k_ref, v_ref, *, half, page_rows):
    peers = recv_ref.shape[0]

    def one_peer(peer, carry):
        for side in range(2):
            at = info_ref[2 * peer + side] * page_rows + side * half * page_rows
            at = pl.multiple_of(at, page_rows)
            k_ref[pl.ds(at, page_rows), :] = recv_ref[peer, pl.ds(side * page_rows, page_rows), :]
            v_ref[pl.ds(at, page_rows), :] = recv_ref[
                peer, pl.ds((2 + side) * page_rows, page_rows), :
            ]
        return carry

    lax.fori_loop(0, peers, one_peer, 0)


def attend_kernel(
    start_ref,
    recv_ref,
    turn_ref,
    kv_ref,
    other_ref,
    msg_ref,
    s_even,
    s_odd,
    stat_ref,
    *,
    factor,
    keys_at_once,
):
    peers, _, dim = kv_ref.shape
    recent_keys = turn_ref.shape[0]
    length = recent_keys * peers // CORES
    own = length // peers
    parts = (recv_ref.shape[2] - kv_ref.shape[1]) // recent_keys
    heads = CORES * parts
    kv_rows = (kv_ref.shape[1] - INFO_ROWS) // 2
    per_chunk = keys_at_once // kv_rows
    places = [(ref, c) for ref in (kv_ref, other_ref) for c in range(peers // per_chunk)]
    log_factor = factor * math.log2(math.e)
    contract = (((1,), (1,)), ((), ()))
    start = start_ref[0]
    turn_k = turn_ref[:, heads * dim : (heads + 1) * dim]
    turn_v = turn_ref[:, (heads + 1) * dim :]
    lane = lax.broadcasted_iota(jnp.int32, (length, dim), 1)
    token = lax.broadcasted_iota(jnp.int32, (length, recent_keys), 0)
    turn_key = start + lax.broadcasted_iota(jnp.int32, (length, recent_keys), 1)
    visible = turn_key <= token

    def chunk(place, first_row):
        ref, c = place
        rows = ref[c * per_chunk : (c + 1) * per_chunk, first_row : first_row + kv_rows, :]
        return rows.reshape(keys_at_once, dim)

    def scores(head, s_ref):
        first = kv_ref.shape[1] + head % parts * recent_keys
        query = recv_ref[:, head // parts, first : first + recent_keys, :].reshape(length, dim)
        peak = None
        for n, place in enumerate(places):
            s = lax.dot_general(query, chunk(place, 0), contract, preferred_element_type=F32)
            s_ref[:, n * keys_at_once : (n + 1) * keys_at_once] = s
            for i in range(keys_at_once // dim):
                part = s[:, i * dim : (i + 1) * dim]
                peak = part if peak is None else jnp.maximum(peak, part)
        recent = lax.dot_general(query, turn_k, contract, preferred_element_type=F32)
        recent = jnp.where(visible, recent, -jnp.inf)
        top = jnp.maximum(
            jnp.max(peak, axis=1, keepdims=True), jnp.max(recent, axis=1, keepdims=True)
        )
        shift = (top * log_factor).astype(BF16).astype(F32)
        return recent, shift

    def weights(head, s_ref, recent, shift):
        e = jnp.exp2(recent * log_factor - shift)
        total = jnp.sum(e, axis=1, keepdims=True)
        mixed = jnp.dot(e.astype(BF16), turn_v, preferred_element_type=F32)
        spread = jnp.broadcast_to(shift, (length, dim))
        sums = None
        for n, place in enumerate(places):
            parts = []
            for i in range(keys_at_once // dim):
                at = n * keys_at_once + i * dim
                part = jnp.exp2(s_ref[:, at : at + dim] * log_factor - spread)
                sums = part if sums is None else sums + part
                parts.append(part.astype(BF16))
            mixed = mixed + jnp.dot(
                jnp.concatenate(parts, axis=1), chunk(place, kv_rows), preferred_element_type=F32
            )
        total = total + jnp.sum(sums, axis=1, keepdims=True)
        high = total.astype(BF16).astype(F32)
        stat = stat_ref[...]
        stat = jnp.where(lane == head, shift, stat)
        stat = jnp.where(lane == heads + head, high, stat)
        stat = jnp.where(lane == 2 * heads + head, total - high, stat)
        stat_ref[...] = stat
        msg_ref[:, head * own : (head + 1) * own, :] = mixed.astype(BF16).reshape(
            peers, own, dim
        )

    stat_ref[...] = jnp.zeros((length, dim), F32)
    held = scores(0, s_even)
    for head in range(heads):
        now, later = (s_even, s_odd) if head % 2 == 0 else (s_odd, s_even)
        coming = scores(head + 1, later) if head + 1 < heads else None
        weights(head, now, *held)
        held = coming
    msg_ref[:, heads * own :, :] = stat_ref[...].astype(BF16).reshape(peers, own, dim)


def combine_kernel(msg_ref, out_ref):
    peers, rows, dim = msg_ref.shape
    own = out_ref.shape[0]
    heads = rows // own - 1
    keep = lax.broadcasted_iota(jnp.int32, (own, dim), 1) < heads
    for share in range(CORES):
        senders = range(share, peers, CORES)
        stats = [msg_ref[p, heads * own :, :].astype(F32) for p in senders]
        top = stats[0]
        for stat in stats[1:]:
            top = jnp.maximum(top, stat)
        factors, total = [], jnp.zeros((own, dim), F32)
        for stat in stats:
            w = jnp.exp2(jnp.where(keep, stat - top, 0.0))
            sums = pltpu.roll(stat, dim - heads, 1) + pltpu.roll(stat, dim - 2 * heads, 1)
            total = total + w * sums
            factors.append(w)
        total = jnp.where(keep, total, 1.0)
        factors = [w / total for w in factors]
        for h in range(heads):
            acc = None
            for p, w in zip(senders, factors):
                part = msg_ref[p, h * own : (h + 1) * own, :].astype(F32) * w[:, h : h + 1]
                acc = part if acc is None else acc + part
            at = (share * heads + h) * dim
            out_ref[:, at : at + dim] = acc.astype(BF16)


def whole(memory_space=pltpu.VMEM):
    return pl.BlockSpec(memory_space=memory_space)


def near(x):
    return pltpu.with_memory_space_constraint(x, pltpu.VMEM)


def step(q_turn, k_turn, v_turn, cache_k, cache_v, k_scale, v_scale, page_map):
    ctx = ("y", "core")
    peers = lax.axis_size(ctx)
    groups = lax.axis_size("head")
    slots, page_rows, dim = cache_k.shape
    half = slots // 2
    tokens = q_turn.shape[0]
    chip_tokens = tokens * groups * CORES
    own = tokens * groups
    length = own * peers
    width = q_turn.shape[1] // groups
    share = width // CORES
    heads = share // dim
    kv_rows = 4 * page_rows + INFO_ROWS
    rows = kv_rows + chip_tokens * heads // CORES
    smem = whole(pltpu.SMEM)
    vmem = whole()

    turn = pl.pallas_call(
        lambda *refs: pack_kernel(*refs, groups=groups),
        out_shape=jax.ShapeDtypeStruct((CORES * groups, tokens, share + 2 * dim), BF16),
        in_specs=[vmem, vmem, vmem],
        out_specs=vmem,
        name="pack",
    )(q_turn, k_turn, v_turn)
    turn = lax.all_to_all(turn, ("core", "head"), split_axis=0, concat_axis=0, tiled=True)
    turn = near(turn.reshape(chip_tokens, share + 2 * dim))

    prepare = pl.pallas_call(
        lambda *refs: prepare_kernel(*refs, half=half, peers=peers),
        out_shape=pltpu.VMEM((peers, kv_rows, dim), BF16),
        in_specs=[smem, smem, smem, vmem, vmem],
        out_specs=vmem,
        name="prepare",
    )
    kv = prepare(page_map, k_scale.reshape(slots), v_scale.reshape(slots), cache_k, cache_v)
    other = lax.ppermute(kv, "core", [(i, CORES - 1 - i) for i in range(CORES)])
    kv, other = lax.optimization_barrier((kv, other))
    kv, other = near(kv), pltpu.with_memory_space_constraint(other, pltpu.HBM)

    filled = pl.pallas_call(
        fill_kernel,
        out_shape=jax.ShapeDtypeStruct((peers, rows, dim), BF16),
        in_specs=[vmem, vmem],
        out_specs=vmem,
        name="fill",
    )(turn, kv)
    recv = lax.all_to_all(filled, ctx, split_axis=0, concat_axis=0, tiled=True)

    attend = pl.pallas_call(
        lambda *refs: attend_kernel(*refs, factor=1.0 / math.sqrt(dim), keys_at_once=512),
        out_shape=jax.ShapeDtypeStruct((peers, (heads + 1) * own, dim), BF16),
        in_specs=[smem, vmem, vmem, vmem, vmem],
        out_specs=vmem,
        scratch_shapes=[
            pltpu.VMEM((length, CORES * slots * page_rows), F32),
            pltpu.VMEM((length, CORES * slots * page_rows), F32),
            pltpu.VMEM((length, dim), F32),
        ],
        compiler_params=pltpu.CompilerParams(vmem_limit_bytes=32 << 20),
        name="attend",
    )
    start = (lax.axis_index("y") * chip_tokens).reshape(1).astype(jnp.int32)
    by_core = near(recv.reshape(peers // CORES, CORES, rows, dim))
    msg = attend(start, by_core, turn, kv, other)
    parts = lax.all_to_all(msg, ctx, split_axis=0, concat_axis=0, tiled=True)

    info = recv[:, 4 * page_rows : 4 * page_rows + 2, 0].astype(jnp.int32).reshape(2 * peers)
    paired = jax.ShapeDtypeStruct((slots * page_rows, dim), BF16)
    place = pl.pallas_call(
        lambda *refs: place_kernel(*refs, half=half, page_rows=page_rows),
        out_shape=(paired, paired),
        in_specs=[smem, vmem],
        out_specs=(vmem, vmem),
        compiler_params=SMALL,
        name="place",
    )
    paired_k, paired_v = place(info, near(recv))
    attn_out = pl.pallas_call(
        combine_kernel,
        out_shape=jax.ShapeDtypeStruct((own, width), BF16),
        in_specs=[vmem],
        out_specs=vmem,
        compiler_params=SMALL,
        name="combine",
    )(near(parts))
    return (attn_out, paired_k, paired_v)


def solution(mesh):
    y_axis = mesh.shape["ctx"] // CORES
    devices = mesh.devices.reshape(y_axis, CORES, *mesh.devices.shape[1:])
    mesh = Mesh(devices, ("y", "core", *mesh.axis_names[1:]))
    turn = P(("rep", "y", "core", "head"), None)
    cache = P(("rep", "y", "core"), None, "head")
    scale = P(("rep", "y", "core"), "head")
    return jax.shard_map(
        step,
        mesh=mesh,
        in_specs=(turn, turn, turn, cache, cache, scale, scale, P(("rep", "y", "core"))),
        out_specs=(scale, scale, scale),
        check_vma=False,
    )
```

```python
import math

import jax
import jax.numpy as jnp
from jax import lax
from jax.experimental import pallas as pl
from jax.experimental.pallas import tpu as pltpu
from jax.sharding import PartitionSpec as P


INFO_ROWS = 16
CORES = 2
BF16 = jnp.bfloat16
F32 = jnp.float32
SMALL = pltpu.CompilerParams(vmem_limit_bytes=16 << 20)


def pack_kernel(q_ref, k_ref, v_ref, out_ref, *, groups):
    dim = k_ref.shape[1] // groups
    share = q_ref.shape[1] // (groups * CORES)
    for group in range(groups):
        keys = k_ref[:, group * dim : (group + 1) * dim]
        values = v_ref[:, group * dim : (group + 1) * dim]
        for core in range(CORES):
            at = (group * CORES + core) * share
            query = q_ref[:, at : at + share]
            for to in range(core * groups + group, out_ref.shape[0], CORES * groups):
                out_ref[to, :, :share] = query
                out_ref[to, :, share : share + dim] = keys
                out_ref[to, :, share + dim :] = values


def prepare_kernel(map_ref, k_scale_ref, v_scale_ref, k_ref, v_ref, send_ref, *, half, peers):
    slots, page_rows, width = k_ref.shape
    body_rows = 4 * page_rows
    row = lax.broadcasted_iota(jnp.int32, (INFO_ROWS, width), 0)

    def one_slot(slot, carry):
        page = map_ref[slot]
        block = page // half
        place = page - block * half
        upper = block >= peers
        owner = jnp.where(upper, 2 * peers - 1 - block, block)
        side = jnp.where(upper, 1, 0)
        at_k = pl.multiple_of(side * page_rows, page_rows)
        at_v = pl.multiple_of((2 + side) * page_rows, page_rows)
        send_ref[owner, pl.ds(at_k, page_rows), :] = (
            k_ref[slot].astype(F32) * k_scale_ref[slot]
        ).astype(BF16)
        send_ref[owner, pl.ds(at_v, page_rows), :] = (
            v_ref[slot].astype(F32) * v_scale_ref[slot]
        ).astype(BF16)
        info = send_ref[owner, body_rows : body_rows + INFO_ROWS, :].astype(F32)
        info = jnp.where(row == side, place.astype(F32), info)
        send_ref[owner, body_rows : body_rows + INFO_ROWS, :] = info.astype(BF16)
        return carry

    send_ref[:, body_rows:, :] = jnp.zeros((peers, INFO_ROWS, width), BF16)
    lax.fori_loop(0, slots, one_slot, 0)


def place_kernel(info_ref, recv_ref, k_ref, v_ref, *, half, page_rows):
    peers = recv_ref.shape[0]

    def one_peer(peer, carry):
        for side in range(2):
            at = info_ref[2 * peer + side] * page_rows + side * half * page_rows
            at = pl.multiple_of(at, page_rows)
            k_ref[pl.ds(at, page_rows), :] = recv_ref[peer, pl.ds(side * page_rows, page_rows), :]
            v_ref[pl.ds(at, page_rows), :] = recv_ref[
                peer, pl.ds((2 + side) * page_rows, page_rows), :
            ]
        return carry

    lax.fori_loop(0, peers, one_peer, 0)


def attend_kernel(
    start_ref, turn_ref, kv_ref, other_ref, msg_ref, s_even, s_odd, stat_ref, *, factor, keys_at_once
):
    peers, _, dim = kv_ref.shape
    length, width = turn_ref.shape
    heads = width // dim - 2
    own = length // peers
    recent_keys = CORES * own
    kv_rows = (kv_ref.shape[1] - INFO_ROWS) // 2
    per_chunk = keys_at_once // kv_rows
    places = [(ref, c) for ref in (kv_ref, other_ref) for c in range(peers // per_chunk)]
    log_factor = factor * math.log2(math.e)
    contract = (((1,), (1,)), ((), ()))
    start = pl.multiple_of(start_ref[0], recent_keys)
    turn_k = turn_ref[pl.ds(start, recent_keys), heads * dim : (heads + 1) * dim]
    turn_v = turn_ref[pl.ds(start, recent_keys), (heads + 1) * dim : (heads + 2) * dim]
    lane = lax.broadcasted_iota(jnp.int32, (length, dim), 1)
    token = lax.broadcasted_iota(jnp.int32, (length, recent_keys), 0)
    turn_key = start + lax.broadcasted_iota(jnp.int32, (length, recent_keys), 1)
    visible = turn_key <= token

    def chunk(place, first_row):
        ref, c = place
        rows = ref[c * per_chunk : (c + 1) * per_chunk, first_row : first_row + kv_rows, :]
        return rows.reshape(keys_at_once, dim)

    def scores(head, s_ref):
        query = turn_ref[:, head * dim : (head + 1) * dim]
        peak = None
        for n, place in enumerate(places):
            s = lax.dot_general(query, chunk(place, 0), contract, preferred_element_type=F32)
            s_ref[:, n * keys_at_once : (n + 1) * keys_at_once] = s
            for i in range(keys_at_once // dim):
                part = s[:, i * dim : (i + 1) * dim]
                peak = part if peak is None else jnp.maximum(peak, part)
        recent = lax.dot_general(query, turn_k, contract, preferred_element_type=F32)
        recent = jnp.where(visible, recent, -jnp.inf)
        top = jnp.maximum(
            jnp.max(peak, axis=1, keepdims=True), jnp.max(recent, axis=1, keepdims=True)
        )
        shift = (top * log_factor).astype(BF16).astype(F32)
        return recent, shift

    def weights(head, s_ref, recent, shift):
        e = jnp.exp2(recent * log_factor - shift)
        total = jnp.sum(e, axis=1, keepdims=True)
        mixed = jnp.dot(e.astype(BF16), turn_v, preferred_element_type=F32)
        spread = jnp.broadcast_to(shift, (length, dim))
        sums = None
        for n, place in enumerate(places):
            parts = []
            for i in range(keys_at_once // dim):
                at = n * keys_at_once + i * dim
                part = jnp.exp2(s_ref[:, at : at + dim] * log_factor - spread)
                sums = part if sums is None else sums + part
                parts.append(part.astype(BF16))
            mixed = mixed + jnp.dot(
                jnp.concatenate(parts, axis=1), chunk(place, kv_rows), preferred_element_type=F32
            )
        total = total + jnp.sum(sums, axis=1, keepdims=True)
        high = total.astype(BF16).astype(F32)
        stat = stat_ref[...]
        stat = jnp.where(lane == head, shift, stat)
        stat = jnp.where(lane == heads + head, high, stat)
        stat = jnp.where(lane == 2 * heads + head, total - high, stat)
        stat_ref[...] = stat
        msg_ref[:, head * own : (head + 1) * own, :] = mixed.astype(BF16).reshape(
            peers, own, dim
        )

    stat_ref[...] = jnp.zeros((length, dim), F32)
    held = scores(0, s_even)
    for head in range(heads):
        now, later = (s_even, s_odd) if head % 2 == 0 else (s_odd, s_even)
        coming = scores(head + 1, later) if head + 1 < heads else None
        weights(head, now, *held)
        held = coming
    msg_ref[:, heads * own :, :] = stat_ref[...].astype(BF16).reshape(peers, own, dim)


def combine_kernel(msg_ref, out_ref):
    peers, rows, dim = msg_ref.shape
    own = out_ref.shape[0]
    heads = rows // own - 1
    keep = lax.broadcasted_iota(jnp.int32, (own, dim), 1) < heads
    for share in range(CORES):
        senders = range(share, peers, CORES)
        stats = [msg_ref[p, heads * own :, :].astype(F32) for p in senders]
        top = stats[0]
        for stat in stats[1:]:
            top = jnp.maximum(top, stat)
        factors, total = [], jnp.zeros((own, dim), F32)
        for stat in stats:
            w = jnp.exp2(jnp.where(keep, stat - top, 0.0))
            sums = pltpu.roll(stat, dim - heads, 1) + pltpu.roll(stat, dim - 2 * heads, 1)
            total = total + w * sums
            factors.append(w)
        total = jnp.where(keep, total, 1.0)
        factors = [w / total for w in factors]
        for h in range(heads):
            acc = None
            for p, w in zip(senders, factors):
                part = msg_ref[p, h * own : (h + 1) * own, :].astype(F32) * w[:, h : h + 1]
                acc = part if acc is None else acc + part
            at = (share * heads + h) * dim
            out_ref[:, at : at + dim] = acc.astype(BF16)


def whole(memory_space=pltpu.VMEM):
    return pl.BlockSpec(memory_space=memory_space)


def near(x):
    return pltpu.with_memory_space_constraint(x, pltpu.VMEM)


def step(q_turn, k_turn, v_turn, cache_k, cache_v, k_scale, v_scale, page_map):
    peers = lax.axis_size("ctx")
    groups = lax.axis_size("head")
    position = lax.axis_index("ctx")
    slots, page_rows, dim = cache_k.shape
    half = slots // 2
    tokens = q_turn.shape[0]
    own = tokens * groups
    length = own * peers
    width = q_turn.shape[1] // groups
    share = width // CORES
    heads = share // dim
    smem = whole(pltpu.SMEM)
    vmem = whole()

    turn = pl.pallas_call(
        lambda *refs: pack_kernel(*refs, groups=groups),
        out_shape=jax.ShapeDtypeStruct((peers * groups, tokens, share + 2 * dim), BF16),
        in_specs=[vmem, vmem, vmem],
        out_specs=vmem,
        name="pack",
    )(q_turn, k_turn, v_turn)
    turn = lax.all_to_all(turn, ("ctx", "head"), split_axis=0, concat_axis=0, tiled=True)

    prepare = pl.pallas_call(
        lambda *refs: prepare_kernel(*refs, half=half, peers=peers),
        out_shape=jax.ShapeDtypeStruct((peers, 4 * page_rows + INFO_ROWS, dim), BF16),
        in_specs=[smem, smem, smem, vmem, vmem],
        out_specs=vmem,
        name="prepare",
    )
    send = prepare(page_map, k_scale.reshape(slots), v_scale.reshape(slots), cache_k, cache_v)
    other = lax.ppermute(send, "ctx", [(i, i ^ 1) for i in range(peers)])
    turn, outgoing = lax.optimization_barrier((turn, send))
    turn = turn.reshape(length, share + 2 * dim)
    recv = lax.all_to_all(outgoing, "ctx", split_axis=0, concat_axis=0, tiled=True)

    attend = pl.pallas_call(
        lambda *refs: attend_kernel(*refs, factor=1.0 / math.sqrt(dim), keys_at_once=512),
        out_shape=jax.ShapeDtypeStruct((peers, (heads + 1) * own, dim), BF16),
        in_specs=[smem, vmem, vmem, vmem],
        out_specs=vmem,
        scratch_shapes=[
            pltpu.VMEM((length, CORES * slots * page_rows), F32),
            pltpu.VMEM((length, CORES * slots * page_rows), F32),
            pltpu.VMEM((length, dim), F32),
        ],
        name="attend",
    )
    start = (position // CORES * (CORES * own)).reshape(1).astype(jnp.int32)
    msg = attend(start, turn, send, other)
    msg, recv = lax.optimization_barrier((msg, recv))
    parts = lax.all_to_all(msg, "ctx", split_axis=0, concat_axis=0, tiled=True)

    info = recv[:, 4 * page_rows : 4 * page_rows + 2, 0].astype(jnp.int32).reshape(2 * peers)
    paired = jax.ShapeDtypeStruct((slots * page_rows, dim), BF16)
    place = pl.pallas_call(
        lambda *refs: place_kernel(*refs, half=half, page_rows=page_rows),
        out_shape=(paired, paired),
        in_specs=[smem, vmem],
        out_specs=(vmem, vmem),
        compiler_params=SMALL,
        name="place",
    )
    paired_k, paired_v = place(info, near(recv))
    attn_out = pl.pallas_call(
        combine_kernel,
        out_shape=jax.ShapeDtypeStruct((own, width), BF16),
        in_specs=[vmem],
        out_specs=vmem,
        compiler_params=SMALL,
        name="combine",
    )(near(parts))
    return (attn_out, paired_k, paired_v)


def solution(mesh):
    return jax.shard_map(
        step,
        mesh=mesh,
        in_specs=(
            P(("rep", "ctx", "head"), None),
            P(("rep", "ctx", "head"), None),
            P(("rep", "ctx", "head"), None),
            P(("rep", "ctx"), None, "head"),
            P(("rep", "ctx"), None, "head"),
            P(("rep", "ctx"), "head"),
            P(("rep", "ctx"), "head"),
            P(("rep", "ctx")),
        ),
        out_specs=(P(("rep", "ctx"), "head"), P(("rep", "ctx"), "head"), P(("rep", "ctx"), "head")),
        check_vma=False,
    )
```

```python
import math

import jax
import jax.numpy as jnp
from jax import lax
from jax.experimental import pallas as pl
from jax.experimental.pallas import tpu as pltpu
from jax.sharding import PartitionSpec as P


INFO_ROWS = 8
CORES = 2
BF16 = jnp.bfloat16
F32 = jnp.float32
SMALL = pltpu.CompilerParams(vmem_limit_bytes=16 << 20)


def pack_kernel(q_ref, k_ref, v_ref, out_ref, block_ref, sems, *, groups):
    dim = k_ref.shape[1] // groups
    share = q_ref.shape[1] // (groups * CORES)
    for core in range(CORES):
        for group in range(groups):
            at = (group * CORES + core) * share
            head = slice(group * dim, (group + 1) * dim)
            block_ref[core * groups + group, :, :share] = q_ref[:, at : at + share]
            block_ref[core * groups + group, 0:1, share:] = k_ref[core : core + 1, head]
            block_ref[core * groups + group, 1:2, share:] = v_ref[core : core + 1, head]
    count = block_ref.shape[0]
    copies = [
        pltpu.make_async_copy(block_ref, out_ref.at[pl.ds(y * count, count)], sems.at[y])
        for y in range(out_ref.shape[0] // count)
    ]
    for copy in copies:
        copy.start()
    for copy in copies:
        copy.wait()


def prepare_kernel(map_ref, k_scale_ref, v_scale_ref, k_ref, v_ref, send_ref, *, half, peers):
    slots, page_rows, width = k_ref.shape
    body_rows = 4 * page_rows
    row = lax.broadcasted_iota(jnp.int32, (INFO_ROWS, width), 0)

    def one_slot(slot, carry):
        page = map_ref[slot]
        block = page // half
        place = page - block * half
        upper = block >= peers
        owner = jnp.where(upper, 2 * peers - 1 - block, block)
        side = jnp.where(upper, 1, 0)
        at_k = pl.multiple_of(side * page_rows, page_rows)
        at_v = pl.multiple_of((2 + side) * page_rows, page_rows)
        send_ref[owner, pl.ds(at_k, page_rows), :] = (
            k_ref[slot].astype(F32) * k_scale_ref[slot]
        ).astype(BF16)
        send_ref[owner, pl.ds(at_v, page_rows), :] = (
            v_ref[slot].astype(F32) * v_scale_ref[slot]
        ).astype(BF16)
        info = send_ref[owner, body_rows : body_rows + INFO_ROWS, :].astype(F32)
        info = jnp.where(row == side, place.astype(F32), info)
        send_ref[owner, body_rows : body_rows + INFO_ROWS, :] = info.astype(BF16)
        return carry

    send_ref[:, body_rows:, :] = jnp.zeros((peers, INFO_ROWS, width), BF16)
    lax.fori_loop(0, slots, one_slot, 0)


def place_kernel(info_ref, recv_ref, k_ref, v_ref, *, half, page_rows):
    peers = recv_ref.shape[0]

    def one_peer(peer, carry):
        for side in range(2):
            at = info_ref[2 * peer + side] * page_rows + side * half * page_rows
            at = pl.multiple_of(at, page_rows)
            k_ref[pl.ds(at, page_rows), :] = recv_ref[peer, pl.ds(side * page_rows, page_rows), :]
            v_ref[pl.ds(at, page_rows), :] = recv_ref[
                peer, pl.ds((2 + side) * page_rows, page_rows), :
            ]
        return carry

    lax.fori_loop(0, peers, one_peer, 0)


def attend_kernel(
    where_ref,
    turn_ref,
    mine_ref,
    theirs_ref,
    kv_ref,
    other_ref,
    msg_ref,
    s_even,
    s_odd,
    stat_ref,
    *,
    factor,
    keys_at_once,
):
    peers, _, dim = kv_ref.shape
    length, width = turn_ref.shape
    heads = width // dim - 1
    own = length // peers
    recent_keys = CORES * own
    kv_rows = (kv_ref.shape[1] - INFO_ROWS) // 2
    per_chunk = keys_at_once // kv_rows
    places = [(ref, c) for ref in (kv_ref, other_ref) for c in range(peers // per_chunk)]
    log_factor = factor * math.log2(math.e)
    contract = (((1,), (1,)), ((), ()))
    start, core = where_ref[0], where_ref[1]
    turn_k = jnp.concatenate([mine_ref[...], theirs_ref[...]], axis=0)
    turn_v = jnp.concatenate(
        [pltpu.roll(ref[...].astype(F32), recent_keys - 1, 0) for ref in (mine_ref, theirs_ref)],
        axis=0,
    ).astype(BF16)
    lane = lax.broadcasted_iota(jnp.int32, (length, dim), 1)
    token = lax.broadcasted_iota(jnp.int32, (length, CORES * recent_keys), 0)
    row = lax.broadcasted_iota(jnp.int32, (length, CORES * recent_keys), 1)
    is_mine = row < recent_keys
    turn_key = jnp.where(is_mine, row + core, row - recent_keys + 1 - core) + start
    visible = jnp.logical_and(row % CORES == 0, turn_key <= token)

    def chunk(place, first_row):
        ref, c = place
        rows = ref[c * per_chunk : (c + 1) * per_chunk, first_row : first_row + kv_rows, :]
        return rows.reshape(keys_at_once, dim)

    def scores(head, s_ref):
        query = turn_ref[:, head * dim : (head + 1) * dim]
        peak = None
        for n, place in enumerate(places):
            s = lax.dot_general(query, chunk(place, 0), contract, preferred_element_type=F32)
            s_ref[:, n * keys_at_once : (n + 1) * keys_at_once] = s
            for i in range(keys_at_once // dim):
                part = s[:, i * dim : (i + 1) * dim]
                peak = part if peak is None else jnp.maximum(peak, part)
        recent = lax.dot_general(query, turn_k, contract, preferred_element_type=F32)
        recent = jnp.where(visible, recent, -jnp.inf)
        top = jnp.maximum(
            jnp.max(peak, axis=1, keepdims=True), jnp.max(recent, axis=1, keepdims=True)
        )
        shift = (top * log_factor).astype(BF16).astype(F32)
        return recent, shift

    def weights(head, s_ref, recent, shift):
        e = jnp.exp2(recent * log_factor - shift)
        total = jnp.sum(e, axis=1, keepdims=True)
        mixed = jnp.dot(e.astype(BF16), turn_v, preferred_element_type=F32)
        spread = jnp.broadcast_to(shift, (length, dim))
        sums = None
        for n, place in enumerate(places):
            parts = []
            for i in range(keys_at_once // dim):
                at = n * keys_at_once + i * dim
                part = jnp.exp2(s_ref[:, at : at + dim] * log_factor - spread)
                sums = part if sums is None else sums + part
                parts.append(part.astype(BF16))
            mixed = mixed + jnp.dot(
                jnp.concatenate(parts, axis=1), chunk(place, kv_rows), preferred_element_type=F32
            )
        total = total + jnp.sum(sums, axis=1, keepdims=True)
        high = total.astype(BF16).astype(F32)
        stat = stat_ref[...]
        stat = jnp.where(lane == head, shift, stat)
        stat = jnp.where(lane == heads + head, high, stat)
        stat = jnp.where(lane == 2 * heads + head, total - high, stat)
        stat_ref[...] = stat
        msg_ref[:, head * own : (head + 1) * own, :] = mixed.astype(BF16).reshape(
            peers, own, dim
        )

    stat_ref[...] = jnp.zeros((length, dim), F32)
    held = scores(0, s_even)
    for head in range(heads):
        now, later = (s_even, s_odd) if head % 2 == 0 else (s_odd, s_even)
        coming = scores(head + 1, later) if head + 1 < heads else None
        weights(head, now, *held)
        held = coming
    msg_ref[:, heads * own :, :] = stat_ref[...].astype(BF16).reshape(peers, own, dim)


def combine_kernel(msg_ref, out_ref):
    peers, rows, dim = msg_ref.shape
    own = out_ref.shape[0]
    heads = rows // own - 1
    keep = lax.broadcasted_iota(jnp.int32, (own, dim), 1) < heads
    for share in range(CORES):
        senders = range(share, peers, CORES)
        stats = [msg_ref[p, heads * own :, :].astype(F32) for p in senders]
        top = stats[0]
        for stat in stats[1:]:
            top = jnp.maximum(top, stat)
        factors, total = [], jnp.zeros((own, dim), F32)
        for stat in stats:
            w = jnp.exp2(jnp.where(keep, stat - top, 0.0))
            sums = pltpu.roll(stat, dim - heads, 1) + pltpu.roll(stat, dim - 2 * heads, 1)
            total = total + w * sums
            factors.append(w)
        total = jnp.where(keep, total, 1.0)
        factors = [w / total for w in factors]
        for h in range(heads):
            acc = None
            for p, w in zip(senders, factors):
                part = msg_ref[p, h * own : (h + 1) * own, :].astype(F32) * w[:, h : h + 1]
                acc = part if acc is None else acc + part
            at = (share * heads + h) * dim
            out_ref[:, at : at + dim] = acc.astype(BF16)


def whole(memory_space=pltpu.VMEM):
    return pl.BlockSpec(memory_space=memory_space)


def near(x):
    return pltpu.with_memory_space_constraint(x, pltpu.VMEM)


def step(q_turn, k_turn, v_turn, cache_k, cache_v, k_scale, v_scale, page_map):
    peers = lax.axis_size("ctx")
    groups = lax.axis_size("head")
    position = lax.axis_index("ctx")
    slots, page_rows, dim = cache_k.shape
    half = slots // 2
    tokens = q_turn.shape[0]
    own = tokens * groups
    length = own * peers
    width = q_turn.shape[1] // groups
    share = width // CORES
    heads = share // dim
    smem = whole(pltpu.SMEM)
    vmem = whole()

    assert tokens == CORES
    turn = pl.pallas_call(
        lambda *refs: pack_kernel(*refs, groups=groups),
        out_shape=jax.ShapeDtypeStruct((peers * groups, tokens, share + dim), BF16),
        in_specs=[vmem, vmem, vmem],
        out_specs=whole(pl.ANY),
        scratch_shapes=[
            pltpu.VMEM((CORES * groups, tokens, share + dim), BF16),
            pltpu.SemaphoreType.DMA((peers // CORES,)),
        ],
        name="pack",
    )(q_turn, k_turn, v_turn)
    turn = lax.all_to_all(turn, ("ctx", "head"), split_axis=0, concat_axis=0, tiled=True)

    prepare = pl.pallas_call(
        lambda *refs: prepare_kernel(*refs, half=half, peers=peers),
        out_shape=jax.ShapeDtypeStruct((peers, 4 * page_rows + INFO_ROWS, dim), BF16),
        in_specs=[smem, smem, smem, vmem, vmem],
        out_specs=vmem,
        name="prepare",
    )
    send = prepare(page_map, k_scale.reshape(slots), v_scale.reshape(slots), cache_k, cache_v)
    other = lax.ppermute(send, "ctx", [(i, i ^ 1) for i in range(peers)])
    turn, outgoing = lax.optimization_barrier((turn, send))
    turn = turn.reshape(length, share + dim)
    start = position // CORES * (CORES * own)
    mine = lax.dynamic_slice(turn, (start, share), (CORES * own, dim))
    theirs = lax.ppermute(mine, "ctx", [(i, i ^ 1) for i in range(peers)])
    recv = lax.all_to_all(outgoing, "ctx", split_axis=0, concat_axis=0, tiled=True)

    attend = pl.pallas_call(
        lambda *refs: attend_kernel(*refs, factor=1.0 / math.sqrt(dim), keys_at_once=512),
        out_shape=jax.ShapeDtypeStruct((peers, (heads + 1) * own, dim), BF16),
        in_specs=[smem, vmem, vmem, vmem, vmem, vmem],
        out_specs=vmem,
        scratch_shapes=[
            pltpu.VMEM((length, CORES * slots * page_rows), F32),
            pltpu.VMEM((length, CORES * slots * page_rows), F32),
            pltpu.VMEM((length, dim), F32),
        ],
        name="attend",
    )
    where = jnp.stack([start, position % CORES]).astype(jnp.int32)
    msg = attend(where, turn, mine, theirs, send, other)
    msg, recv = lax.optimization_barrier((msg, recv))
    parts = lax.all_to_all(msg, "ctx", split_axis=0, concat_axis=0, tiled=True)

    info = recv[:, 4 * page_rows : 4 * page_rows + 2, 0].astype(jnp.int32).reshape(2 * peers)
    paired = jax.ShapeDtypeStruct((slots * page_rows, dim), BF16)
    place = pl.pallas_call(
        lambda *refs: place_kernel(*refs, half=half, page_rows=page_rows),
        out_shape=(paired, paired),
        in_specs=[smem, vmem],
        out_specs=(vmem, vmem),
        compiler_params=SMALL,
        name="place",
    )
    paired_k, paired_v = place(info, near(recv))
    attn_out = pl.pallas_call(
        combine_kernel,
        out_shape=jax.ShapeDtypeStruct((own, width), BF16),
        in_specs=[vmem],
        out_specs=vmem,
        compiler_params=SMALL,
        name="combine",
    )(near(parts))
    return (attn_out, paired_k, paired_v)


def solution(mesh):
    return jax.shard_map(
        step,
        mesh=mesh,
        in_specs=(
            P(("rep", "ctx", "head"), None),
            P(("rep", "ctx", "head"), None),
            P(("rep", "ctx", "head"), None),
            P(("rep", "ctx"), None, "head"),
            P(("rep", "ctx"), None, "head"),
            P(("rep", "ctx"), "head"),
            P(("rep", "ctx"), "head"),
            P(("rep", "ctx")),
        ),
        out_specs=(P(("rep", "ctx"), "head"), P(("rep", "ctx"), "head"), P(("rep", "ctx"), "head")),
        check_vma=False,
    )
```
